512 devices in a mesh: dp: 16 (over y, x), expert: 32 (over z, core).
Axes of the slice: x: 4, y: 4, z: 16, core: 2. Of those that a mesh axis runs over, the one named last changes fastest.
Arguments:
- panorama: bfloat16 [31, 768, 1664], P(None, 'expert', 'dp'), may hold values from -6 to 6
- tile_anchor: int32 [64, 2], P('expert'), may hold values from 0 to 7
- tile_count: int32 [32], P('expert'), may hold values from 1 to 2, as said below
- pre_attention_gain: float32 [1664], P('dp'), may hold values from 0.1 to 1.9
- qkv_weight: bfloat16 [3, 1664, 1664], P(None, None, 'dp'), may hold values from -0.21875 to 0.21875
- out_weight: bfloat16 [1664, 1664], P(None, 'dp'), may hold values from -0.21875 to 0.21875
- pre_expert_gain: float32 [1664], P('dp'), may hold values from 0.1 to 1.9
- router_weight: float32 [1664, 32], P('dp'), may hold values from -0.3125 to 0.3125
- expand_weight: bfloat16 [32, 1664, 8192], P('expert', None, 'dp'), may hold values from -0.15625 to 0.15625
- reduce_weight: bfloat16 [32, 8192, 1664], P('expert', 'dp'), may hold values from -0.09375 to 0.09375
- route_index: int32 [36864, 2], P('expert'), may hold values from 0 to 31, as said below
- slot_index: int32 [36864, 2], P('expert'), may hold values from -1 to 35, as said below
Outputs:
- panorama_out: bfloat16 [31, 768, 1664], P(None, 'expert', 'dp')
The draws below stay inside these ranges and needn't reach their ends.
Inputs may be any that keep to these rules, and one draw needn't show every extreme that they name: `tile_count`: some tile column has 2 live tiles. `route_index`: each token names two different experts. `slot_index`: within one tile column, the kept assignments to one expert have distinct slots; every assignment of a token of a tile slot that is not live is dropped; in every draw one expert holds 36 kept assignments from every tile column.
All inputs are finite; a program needn't handle non-finite values.
Results may differ from the reference program's by a relative error of at most 0.0089.
Values may be sent and summed in bfloat16 or wider, within the bound.
A program may use at most 64 MiB of HBM per device.

```python
import jax
import jax.numpy as jnp
from jax import lax

D = 1664
HEADS = 16
HEAD_DIM = 104
MLP = 8192
EXPERTS = 32
TILE_SIDE = 24
TILE_TOK = 576
TILES_COL = 2
OWN_W = 24
ANCHOR_SPAN = 8
MH = 31
MW = 768
COLS = 32
TILES = 64
TC = 1152
TOKENS = 36864
CAP = 36
N_DP = 16


def make_plan(key):
    base = jax.random.fold_in(key, 11)
    keys = jax.random.split(base, 8)
    counts = jax.random.randint(keys[0], (COLS,), 1, TILES_COL + 1)
    full_column = jax.random.randint(keys[1], (), 0, COLS)
    counts = jnp.where(jnp.arange(COLS) == full_column, TILES_COL, counts).astype(jnp.int32)
    live = jnp.arange(TC)[None, :] // TILE_TOK < counts[:, None]
    popular = jax.random.permutation(keys[2], EXPERTS)
    first_draw = jnp.minimum(jax.random.randint(keys[3], (COLS, TC), 0, EXPERTS), jax.random.randint(keys[4], (COLS, TC), 0, EXPERTS))
    forced_rank = jax.vmap(lambda k: jax.random.permutation(k, TILE_TOK))(jax.random.split(keys[5], COLS))
    forced = jnp.concatenate([forced_rank < CAP, jnp.zeros((COLS, TC - TILE_TOK), bool)], axis=1)
    first = popular[jnp.where(forced, 0, first_draw)]
    second = (first + jax.random.randint(keys[6], (COLS, TC), 1, EXPERTS)) % EXPERTS
    routes = jnp.stack([first, second], axis=-1).astype(jnp.int32)
    priority = jax.vmap(lambda k: jax.random.permutation(k, TC))(jax.random.split(keys[7], COLS))
    ordered_routes = jnp.take_along_axis(routes, priority[:, :, None], axis=1)
    ordered_live = jnp.take_along_axis(live, priority, axis=1)
    listed = jnp.transpose(ordered_routes, (0, 2, 1)).reshape(COLS, 2 * TC)
    listed_live = jnp.concatenate([ordered_live, ordered_live], axis=1)
    onehot = ((listed[:, :, None] == jnp.arange(EXPERTS)[None, None, :]) & listed_live[:, :, None]).astype(jnp.int32)
    before = jnp.cumsum(onehot, axis=1) - onehot
    ranks = jnp.sum(before * onehot, axis=-1).reshape(COLS, 2, TC).transpose(0, 2, 1)
    inverse = jnp.argsort(priority, axis=1)
    token_ranks = jnp.take_along_axis(ranks, inverse[:, :, None], axis=1)
    slots = jnp.where(live[:, :, None] & (token_ranks < CAP), token_ranks, -1).astype(jnp.int32)
    return (counts, routes.reshape(TOKENS, 2), slots.reshape(TOKENS, 2))


def draw_tile_count(key, part):
    return make_plan(key)[0]


def draw_route_index(key, part):
    return make_plan(key)[1]


def draw_slot_index(key, part):
    return make_plan(key)[2]


def touch_ends(entries, own_key, low, top_value):
    longest = entries.shape.index(max(entries.shape))
    spots = []
    for shift in (0, 1):
        where = [jax.random.randint(jax.random.fold_in(own_key, axis), (), 0, length) for axis, length in enumerate(entries.shape)]
        where[longest] = (where[longest] + shift) % entries.shape[longest]
        spots.append(tuple(where))
    return entries.at[spots[0]].set(low).at[spots[1]].set(top_value)


def strengthened(array, stream_key, source, target, blocks, factor):
    owner, partner = [(jnp.arange(array.shape[axis_at]) // (array.shape[axis_at] // blocks)).reshape([-1 if axis == axis_at else 1 for axis in range(array.ndim)]) for axis_at in (source, target)]
    chosen = jax.random.permutation(stream_key, blocks)[partner]
    strong = (owner == chosen) | (owner == (partner + blocks // 2) % blocks)
    return jnp.where(strong, factor * array, array)


def block_levels(stream_key, extent, pieces, low, largest):
    loudness = 1.0
    for axis_at, blocks in pieces:
        steps = jax.random.uniform(jax.random.fold_in(jax.random.fold_in(stream_key, 6), axis_at), (blocks,), jnp.float32, low / len(pieces), largest / len(pieces))
        loudness = loudness * jnp.repeat(jnp.exp(steps), extent[axis_at] // blocks).reshape((-1,) + (1,) * (len(extent) - 1 - axis_at))
    return loudness


def bell_draw(rng, extent, spread, most, pieces=(), held_as=jnp.bfloat16):
    values = spread * jax.random.normal(rng, extent, jnp.float32)
    if pieces:
        values = values * block_levels(rng, extent, pieces, -0.22, 0.18)
    return jnp.clip(values, -most, most).astype(held_as)


def gaussian_with(key, extent, scale, reach, shards, heavy, kind=jnp.bfloat16):
    drawn = scale * jax.random.normal(key, extent, jnp.float32)
    if shards:
        drawn = drawn * block_levels(key, extent, shards, -0.22, 0.18)
    return jnp.clip(strengthened(drawn, jax.random.fold_in(key, 3), *heavy), -reach, reach).astype(kind)


def setup_inputs(seed: int = 0) -> dict:
    key_of = jax.random.split(jax.random.key(seed), 13)
    panorama = bell_draw(key_of[0], (MH, MW, D), 1.0, 6.0, ((1, 32), (2, 16)))
    tile_anchor = touch_ends(jax.random.randint(key_of[1], (TILES, 2), 0, ANCHOR_SPAN), jax.random.fold_in(key_of[1], 1), 0, ANCHOR_SPAN - 1).astype(jnp.int32)
    tile_count = draw_tile_count(jax.random.fold_in(key_of[12], 71), 0)
    pre_attention_gain = jnp.clip(1.0 + 0.18 * jax.random.normal(key_of[3], (D,), jnp.float32), 0.1, 1.9)
    qkv_weight = gaussian_with(key_of[4], (3, D, D), D ** -0.5, 0.21875, ((2, 16),), (1, 2, 16, 2.0))
    out_weight = gaussian_with(key_of[5], (D, D), D ** -0.5, 0.21875, ((1, 16),), (0, 1, 16, 2.0))
    pre_expert_gain = jnp.clip(1.0 + 0.18 * jax.random.normal(key_of[6], (D,), jnp.float32), 0.1, 1.9)
    router_weight = bell_draw(key_of[7], (D, EXPERTS), (D // 4) ** -0.5, 0.3125, ((0, 16),), jnp.float32)
    expand_weight = bell_draw(key_of[8], (EXPERTS, D, MLP), D ** -0.5, 0.15625, ((0, 32), (2, 16)))
    reduce_weight = gaussian_with(key_of[9], (EXPERTS, MLP, D), MLP ** -0.5, 0.09375, ((0, 32), (1, 16)), (1, 2, 16, 2.0))
    route_index = draw_route_index(jax.random.fold_in(key_of[12], 71), 0)
    slot_index = draw_slot_index(jax.random.fold_in(key_of[12], 71), 0)
    return dict(panorama=panorama, tile_anchor=tile_anchor, tile_count=tile_count, pre_attention_gain=pre_attention_gain, qkv_weight=qkv_weight, out_weight=out_weight, pre_expert_gain=pre_expert_gain, router_weight=router_weight, expand_weight=expand_weight, reduce_weight=reduce_weight, route_index=route_index, slot_index=slot_index)


def normalize(values, gain):
    mean_value = lax.optimization_barrier(jnp.mean(values, axis=-1, keepdims=True))
    variance = lax.optimization_barrier(jnp.mean(values * values, axis=-1, keepdims=True)) - mean_value * mean_value
    return (values - mean_value) * lax.rsqrt(variance + 1e-06) * gain

def tile_attention(block):
    query_tile, key_tile, value_tile = block
    shape = (TILE_TOK, HEADS, HEAD_DIM)
    scores = jnp.einsum('qhd,khd->hqk', query_tile.reshape(shape).astype(jnp.float32), key_tile.reshape(shape).astype(jnp.float32), precision=lax.Precision.HIGHEST) * HEAD_DIM ** (-0.5)
    weights = jnp.exp(scores)
    weights = (weights / lax.optimization_barrier(jnp.sum(weights, axis=-1, keepdims=True))).astype(jnp.bfloat16)
    attended = jnp.einsum('hqk,khd->qhd', weights.astype(jnp.float32), value_tile.reshape(shape).astype(jnp.float32), precision=lax.Precision.HIGHEST)
    return attended.astype(jnp.bfloat16).reshape(TILE_TOK, D)

def run_expert(block):
    rows_in, first_layer, second_layer = block
    hidden_pre = jnp.dot(rows_in, first_layer, preferred_element_type=jnp.float32)
    activated = jax.nn.gelu(hidden_pre, approximate=False).astype(jnp.bfloat16)
    split_act = activated.reshape(COLS * CAP, N_DP, MLP // N_DP).astype(jnp.float32)
    split_weight = second_layer.reshape(N_DP, MLP // N_DP, D).astype(jnp.float32)
    partial_out = jnp.einsum('sbh,bhd->bsd', split_act, split_weight, precision=lax.Precision.HIGHEST).astype(jnp.bfloat16)
    return lax.optimization_barrier(jnp.sum(partial_out.astype(jnp.float32), axis=0)).astype(jnp.bfloat16)

def reference(panorama, tile_anchor, tile_count, pre_attention_gain, qkv_weight, out_weight, pre_expert_gain, router_weight, expand_weight, reduce_weight, route_index, slot_index):
    tile_ids = jnp.arange(TILES, dtype=jnp.int32)
    column = tile_ids // TILES_COL
    live_tile = tile_ids % TILES_COL < tile_count[column]
    step_ids = jnp.arange(TILE_TOK, dtype=jnp.int32)
    patch_rows = tile_anchor[:, 0:1] + (step_ids // TILE_SIDE)[None, :]
    patch_cols = (column[:, None] * OWN_W + tile_anchor[:, 1:2] + (step_ids % TILE_SIDE)[None, :]) % MW
    flat_index = (patch_rows * MW + patch_cols).reshape(TOKENS).astype(jnp.int32)
    live_token = jnp.repeat(live_tile, TILE_TOK)
    tokens = panorama.reshape(MH * MW, D)[flat_index]
    normed = normalize(tokens.astype(jnp.float32), pre_attention_gain).astype(jnp.bfloat16)
    queries = jnp.dot(normed, qkv_weight[0], preferred_element_type=jnp.float32).astype(jnp.bfloat16)
    keys_all = jnp.dot(normed, qkv_weight[1], preferred_element_type=jnp.float32).astype(jnp.bfloat16)
    values_all = jnp.dot(normed, qkv_weight[2], preferred_element_type=jnp.float32).astype(jnp.bfloat16)
    attended = lax.map(tile_attention, (queries.reshape(TILES, TILE_TOK, D), keys_all.reshape(TILES, TILE_TOK, D), values_all.reshape(TILES, TILE_TOK, D))).reshape(TOKENS, D)
    mixed = tokens.astype(jnp.float32) + jnp.dot(attended, out_weight, preferred_element_type=jnp.float32)
    expert_in32 = normalize(mixed, pre_expert_gain)
    logits_all = jnp.dot(expert_in32, router_weight, precision=lax.Precision.HIGHEST)
    chosen = jnp.take_along_axis(logits_all, route_index, axis=1)
    gates = jax.nn.sigmoid(chosen - chosen[:, ::-1])
    expert_in = expert_in32.astype(jnp.bfloat16)
    token_column = jnp.arange(TOKENS, dtype=jnp.int32) // TC
    keep = slot_index >= 0
    total_slots = EXPERTS * COLS * CAP
    target = jnp.where(keep, (route_index * COLS + token_column[:, None]) * CAP + slot_index, total_slots).astype(jnp.int32)
    sources = jnp.broadcast_to(expert_in[:, None, :], (TOKENS, 2, D)).reshape(TOKENS * 2, D)
    packed = jnp.zeros((total_slots + 1, D), jnp.bfloat16).at[target.reshape(-1)].set(sources)[:total_slots]
    packed = packed.reshape(EXPERTS, COLS * CAP, D)
    expert_out = lax.map(run_expert, (packed, expand_weight, reduce_weight)).reshape(total_slots, D)
    fetched = expert_out[jnp.where(keep, target, 0)].astype(jnp.float32)
    weight = jnp.where(keep, gates, 0.0)
    final = mixed + lax.optimization_barrier(jnp.sum(fetched * weight[:, :, None], axis=1))
    out_index = jnp.where(live_token, flat_index, MH * MW).astype(jnp.int32)
    summed = jnp.zeros((MH * MW + 1, D), jnp.float32).at[out_index].add(final)[:MH * MW]
    return summed.reshape(MH, MW, D).astype(jnp.bfloat16)
```

```python
import functools

import jax
import jax.numpy as jnp
from jax import lax
from jax.experimental import pallas as pl
from jax.experimental.pallas import tpu as pltpu
from jax.sharding import Mesh
from jax.sharding import PartitionSpec as P

HEAD_DIM = 104
TILE_SIDE = 24
SIDE = 4
SPAN = 7
DP = ("y", "x")
MESH = pl.DeviceIdType.MESH
BF16 = jnp.bfloat16
F32 = jnp.float32
STEPS = (0, -1, 1, 2)


def near(axis, distance):
    return lax.rem(lax.axis_index(axis) + distance + SIDE, SIDE)


def block_at(primary, along, across):
    if primary == "x":
        return near("y", across) * SIDE + near("x", along)
    return near("y", along) * SIDE + near("x", across)


def greet_neighbours():
    barrier = pltpu.get_barrier_semaphore()
    for axis in DP:
        for step in (1, -1):
            pl.semaphore_signal(
                barrier, inc=1, device_id={axis: near(axis, step)}, device_id_type=MESH
            )
    pl.semaphore_wait(barrier, 4)


def chunks_of(lanes):
    first = (lanes // 128 + 1) // 2 * 128
    return (("x", "y", pl.ds(0, first)), ("y", "x", pl.ds(first, lanes - first)))


def row_halves(rows):
    low = rows // 2 // 16 * 16
    return (pl.ds(0, low), pl.ds(low, rows - low))


def gather_kernel(x_ref, out_ref, local_sem, send_sem, recv_sem):
    rows, lanes = x_ref.shape
    chunks = chunks_of(lanes)
    halves = row_halves(rows)
    own = pltpu.make_async_copy(x_ref, out_ref.at[block_at("x", 0, 0)], local_sem)
    own.start()
    greet_neighbours()
    own.wait()
    sent = []

    def copy_of(c, group, way, step, along, across):
        primary, secondary, span = chunks[c]
        axis = primary if group == 0 else secondary
        part = pl.ds(0, rows) if step == 0 else halves[way ^ c]
        ref = out_ref.at[block_at(primary, along, across), part, span]
        return pltpu.make_async_remote_copy(
            src_ref=ref,
            dst_ref=ref,
            send_sem=send_sem.at[c, group, way, step],
            recv_sem=recv_sem.at[c, group, way, step],
            device_id={axis: near(axis, 1 - 2 * way)},
            device_id_type=MESH,
        )

    def send(*which):
        copy = copy_of(*which)
        copy.start()
        sent.append(copy)

    def arrive(*which):
        copy_of(*which).wait_recv()

    for c in (0, 1):
        for way in (0, 1):
            send(c, 0, way, 0, 0, 0)
    for c in (0, 1):
        for way in (0, 1):
            send(c, 1, way, 0, 0, 0)
    for way in (0, 1):
        for c in (0, 1):
            back = 2 * way - 1
            arrive(c, 0, way, 0, back, 0)
            send(c, 0, way, 1, back, 0)
            for turn in (0, 1):
                send(c, 2 + way, turn, 0, back, 0)
    for way in (0, 1):
        for c in (0, 1):
            back = 2 * way - 1
            arrive(c, 1, way, 0, 0, back)
            send(c, 1, way, 1, 0, back)
    for c in (0, 1):
        for way in (0, 1):
            arrive(c, 0, way, 1, 2, 0)
        for turn in (0, 1):
            send(c, 4, turn, 0, 2, 0)
    for group in (2, 3, 4):
        for way in (0, 1):
            for c in (0, 1):
                along = STEPS[group - 1]
                back = 2 * way - 1
                arrive(c, group, way, 0, along, back)
                send(c, group, way, 1, along, back)
    for group in (1, 2, 3, 4):
        for way in (0, 1):
            for c in (0, 1):
                arrive(c, group, way, 1, STEPS[group - 1], 2)
    for copy in sent:
        copy.wait_send()


def from_group(x, ident):
    rows, lanes = x.shape
    return pl.pallas_call(
        gather_kernel,
        out_shape=jax.ShapeDtypeStruct((SIDE * SIDE, rows, lanes), x.dtype),
        in_specs=[pl.BlockSpec(memory_space=pl.ANY)],
        out_specs=pl.BlockSpec(memory_space=pltpu.VMEM),
        scratch_shapes=[
            pltpu.SemaphoreType.DMA,
            pltpu.SemaphoreType.DMA((2, 5, 2, 2)),
            pltpu.SemaphoreType.DMA((2, 5, 2, 2)),
        ],
        compiler_params=pltpu.CompilerParams(
            collective_id=ident, has_side_effects=True, vmem_limit_bytes=48 << 20
        ),
        name=f"gather_{ident}",
    )(x)


def reduce_kernel(part_ref, out_ref, mid_ref, sum_ref, in_ref, red_ref, send_sem, recv_sem):
    blocks, rows, lanes = part_ref.shape
    chunks = chunks_of(lanes)
    halves = row_halves(rows)
    sent = []
    greet_neighbours()

    def own_ref(c, group, along, across):
        primary, _, span = chunks[c]
        if group:
            return part_ref.at[block_at(primary, along, across), :, span]
        return red_ref.at[c, STEPS.index(along), :, pl.ds(0, span.size)]

    def copy_of(c, group, way, step, src):
        primary, secondary, span = chunks[c]
        axis = secondary if group else primary
        half = halves[way] if step != 1 else halves[1 - way]
        width = pl.ds(0, span.size)
        if step == 0:
            dst = mid_ref.at[c, group, way, pl.ds(0, half.size), width]
        else:
            dst = in_ref.at[c, group, way, half, width]
        return pltpu.make_async_remote_copy(
            src_ref=dst if src is None else src,
            dst_ref=dst,
            send_sem=send_sem.at[c, group, way, step],
            recv_sem=recv_sem.at[c, group, way, step],
            device_id={axis: near(axis, 1 - 2 * way)},
            device_id_type=MESH,
        )

    def send(c, group, way, step, src):
        copy = copy_of(c, group, way, step, src)
        copy.start()
        sent.append(copy)

    def block(c, group, along_step):
        if group:
            return own_ref(c, group, STEPS[group - 1], along_step)
        return own_ref(c, group, along_step, 0)

    def first_part(c, group):
        for way in (0, 1):
            send(c, group, way, 0, block(c, group, 2).at[halves[way]])
        for way in (0, 1):
            send(c, group, way, 1, block(c, group, 1 - 2 * way).at[halves[1 - way]])

    def second_part(c, group):
        width = pl.ds(0, chunks[c][2].size)
        for way in (0, 1):
            half = halves[way]
            size = pl.ds(0, half.size)
            copy_of(c, group, way, 0, None).wait_recv()
            mine = block(c, group, 1 - 2 * way)[half, :].astype(F32)
            sum_ref[c, group, way, size, width] = (
                mine + mid_ref[c, group, way, size, width].astype(F32)
            ).astype(sum_ref.dtype)
            send(c, group, way, 2, sum_ref.at[c, group, way, size, width])

    def total(c, group):
        width = pl.ds(0, chunks[c][2].size)
        for way in (0, 1):
            copy_of(c, group, way, 1, None).wait_recv()
            copy_of(c, group, way, 2, None).wait_recv()
        mine = block(c, group, 0)[...].astype(F32)
        return (
            mine
            + in_ref[c, group, 0, :, width].astype(F32)
            + in_ref[c, group, 1, :, width].astype(F32)
        )

    order = (4, 2, 3, 1)
    for group in order:
        for c in (0, 1):
            first_part(c, group)
    for group in order:
        for c in (0, 1):
            second_part(c, group)
    for group in order:
        for c in (0, 1):
            red_ref[c, group - 1, :, pl.ds(0, chunks[c][2].size)] = total(c, group).astype(
                red_ref.dtype
            )
            if group == 4:
                for way in (0, 1):
                    send(c, 0, way, 0, block(c, 0, 2).at[halves[way]])
            elif group != 1:
                way = 0 if group == 3 else 1
                send(c, 0, way, 1, block(c, 0, 1 - 2 * way).at[halves[1 - way]])
    for c in (0, 1):
        second_part(c, 0)
    for c in (0, 1):
        out_ref[:, chunks[c][2]] = total(c, 0).astype(out_ref.dtype)
    for copy in sent:
        copy.wait_send()


def sum_at_owner(part, ident):
    blocks, rows, lanes = part.shape
    widest = chunks_of(lanes)[0][2].size
    half = row_halves(rows)[1].size
    return pl.pallas_call(
        reduce_kernel,
        out_shape=jax.ShapeDtypeStruct((rows, lanes), part.dtype),
        in_specs=[pl.BlockSpec(memory_space=pltpu.VMEM)],
        out_specs=pl.BlockSpec(memory_space=pltpu.VMEM),
        scratch_shapes=[
            pltpu.VMEM((2, 5, 2, half, widest), part.dtype),
            pltpu.VMEM((2, 5, 2, half, widest), part.dtype),
            pltpu.VMEM((2, 5, 2, rows, widest), part.dtype),
            pltpu.VMEM((2, 4, rows, widest), part.dtype),
            pltpu.SemaphoreType.DMA((2, 5, 2, 3)),
            pltpu.SemaphoreType.DMA((2, 5, 2, 3)),
        ],
        compiler_params=pltpu.CompilerParams(
            collective_id=ident, has_side_effects=True, vmem_limit_bytes=48 << 20
        ),
        name=f"reduce_{ident}",
    )(part)


def exchange_order(count):
    ring = count // 2
    return sorted(range(1, count), key=lambda d: -min(d // 2, ring - d // 2))


def exchange_kernel(x_ref, out_ref, local_sem, send_sem, recv_sem):
    count = x_ref.shape[0]
    me = lax.axis_index("expert")
    barrier = pltpu.get_barrier_semaphore()
    for d in range(1, count):
        pl.semaphore_signal(
            barrier,
            inc=1,
            device_id={"expert": lax.rem(me + d, count)},
            device_id_type=MESH,
        )
    own = pltpu.make_async_copy(x_ref.at[me], out_ref.at[me], local_sem)
    own.start()
    pl.semaphore_wait(barrier, count - 1)
    sent = []
    for d in exchange_order(count):
        peer = lax.rem(me + d, count)
        copy = pltpu.make_async_remote_copy(
            src_ref=x_ref.at[peer],
            dst_ref=out_ref.at[me],
            send_sem=send_sem.at[d],
            recv_sem=recv_sem.at[d],
            device_id={"expert": peer},
            device_id_type=MESH,
        )
        copy.start()
        sent.append(copy)
    own.wait()
    for d in exchange_order(count):
        source = lax.rem(me - d + count, count)
        pltpu.make_async_remote_copy(
            src_ref=x_ref.at[source],
            dst_ref=out_ref.at[source],
            send_sem=send_sem.at[d],
            recv_sem=recv_sem.at[d],
            device_id={"expert": source},
            device_id_type=MESH,
        ).wait_recv()
    for copy in sent:
        copy.wait_send()


def exchanged(x, ident):
    count = x.shape[0]
    return pl.pallas_call(
        exchange_kernel,
        out_shape=jax.ShapeDtypeStruct(x.shape, x.dtype),
        in_specs=[pl.BlockSpec(memory_space=pltpu.VMEM)],
        out_specs=pl.BlockSpec(memory_space=pltpu.VMEM),
        scratch_shapes=[
            pltpu.SemaphoreType.DMA,
            pltpu.SemaphoreType.DMA((count,)),
            pltpu.SemaphoreType.DMA((count,)),
        ],
        compiler_params=pltpu.CompilerParams(collective_id=ident, has_side_effects=True),
        name=f"exchange_{ident}",
    )(x)


def sums_kernel(x_ref, out_ref, mid_ref, in_ref, send_sem, recv_sem):
    barrier = pltpu.get_barrier_semaphore()
    for axis in DP:
        for d in (1, 2, 3):
            pl.semaphore_signal(
                barrier, inc=1, device_id={axis: near(axis, d)}, device_id_type=MESH
            )
    pl.semaphore_wait(barrier, 6)
    for phase, axis in enumerate(("x", "y")):
        src = x_ref if phase == 0 else mid_ref
        copies = []
        for d in (2, 1, 3):
            copy = pltpu.make_async_remote_copy(
                src_ref=src,
                dst_ref=in_ref.at[phase, d],
                send_sem=send_sem.at[phase, d],
                recv_sem=recv_sem.at[phase, d],
                device_id={axis: near(axis, d)},
                device_id_type=MESH,
            )
            copy.start()
            copies.append(copy)
        for copy in copies:
            copy.wait()
        result = src[...] + in_ref[phase, 1] + in_ref[phase, 2] + in_ref[phase, 3]
        if phase == 0:
            mid_ref[...] = result
        else:
            out_ref[...] = result


def summed(x, ident):
    return pl.pallas_call(
        sums_kernel,
        out_shape=jax.ShapeDtypeStruct(x.shape, x.dtype),
        in_specs=[pl.BlockSpec(memory_space=pltpu.VMEM)],
        out_specs=pl.BlockSpec(memory_space=pltpu.VMEM),
        scratch_shapes=[
            pltpu.VMEM(x.shape, x.dtype),
            pltpu.VMEM((2, 4, *x.shape), x.dtype),
            pltpu.SemaphoreType.DMA((2, 4)),
            pltpu.SemaphoreType.DMA((2, 4)),
        ],
        compiler_params=pltpu.CompilerParams(collective_id=ident, has_side_effects=True),
        name=f"sums_{ident}",
    )(x)


def passed_along(block, axis, distance):
    size = lax.axis_size(axis)
    return lax.ppermute(block, axis, [((i - distance) % size, i) for i in range(size)])


def two_parts(x):
    high = x.astype(BF16)
    return high, (x - high.astype(F32)).astype(BF16)


def three_parts(x):
    high, rest = x.astype(BF16), x
    rest = x - high.astype(F32)
    middle = rest.astype(BF16)
    return high, middle, (rest - middle.astype(F32)).astype(BF16)


def body(
    panorama,
    tile_anchor,
    tile_count,
    pre_attention_gain,
    qkv_weight,
    out_weight,
    pre_expert_gain,
    router_weight,
    expand_weight,
    reduce_weight,
    route_index,
    slot_index,
):
    expert_count = lax.axis_size("expert")
    height, own_width, features = panorama.shape
    group = SIDE * SIDE
    full_width = features * group
    tiles_here = tile_anchor.shape[0]
    tile_tokens = TILE_SIDE * TILE_SIDE
    column_tokens = tiles_here * tile_tokens
    experts = router_weight.shape[1]
    capacity = column_tokens // experts
    stride = (capacity + 7) // 8 * 8
    own_patches = height * own_width
    own_lanes = (own_patches + 3 + 127) // 128 * 128
    side_patches = height * SPAN
    side_lanes = (side_patches + 127) // 128 * 128

    across = jnp.transpose(panorama, (2, 1, 0)).reshape(features, own_patches)
    gain_columns = jnp.stack(three_parts(pre_attention_gain), axis=1)
    sent = jnp.concatenate(
        [across, gain_columns, jnp.zeros((features, own_lanes - own_patches - 3), BF16)], axis=1
    )
    side_raw = passed_along(across[:, :side_patches], "expert", -1)
    raw = from_group(sent, 1).reshape(full_width, own_lanes)
    raw32 = raw.astype(F32)
    gain = jnp.sum(raw32[:, own_patches : own_patches + 3], axis=1, keepdims=True)
    mean_value = jnp.sum(raw32, axis=0, keepdims=True) / full_width
    square_value = jnp.sum(raw32 * raw32, axis=0, keepdims=True) / full_width
    inverse_std = lax.rsqrt(square_value - mean_value * mean_value + 1e-06)
    normed = ((raw32 - mean_value) * inverse_std * gain).astype(BF16)
    projected = jnp.einsum("sfo,ft->sot", qkv_weight, normed, preferred_element_type=F32).astype(
        BF16
    )
    side = passed_along(projected[:, :, :side_patches], "expert", -1)
    pad = ((0, 0), (0, 0), (0, side_lanes - side_patches))
    area = jnp.concatenate([projected, jnp.pad(side, pad)], axis=2)
    raw_area = jnp.concatenate([sent, jnp.pad(side_raw, pad[1:])], axis=1)

    step_ids = jnp.arange(tile_tokens, dtype=jnp.int32)
    patch_rows = tile_anchor[:, 0:1] + (step_ids // TILE_SIDE)[None, :]
    patch_cols = tile_anchor[:, 1:2] + (step_ids % TILE_SIDE)[None, :]
    flat = jnp.where(
        patch_cols < own_width,
        patch_cols * height + patch_rows,
        own_lanes + (patch_cols - own_width) * height + patch_rows,
    ).reshape(column_tokens)
    live_tile = jnp.arange(tiles_here, dtype=jnp.int32) < tile_count[0]
    live = jnp.repeat(live_tile, tile_tokens)
    area_ids = jnp.arange(own_lanes + side_lanes, dtype=jnp.int32)
    chosen_patch = (area_ids[:, None] == flat[None, :]).astype(BF16)

    tokens = jnp.dot(raw_area, chosen_patch, preferred_element_type=F32)
    shaped = jnp.einsum("sop,pn->son", area, chosen_patch, preferred_element_type=F32).astype(BF16)
    shaped = shaped.reshape(3, features, tiles_here, tile_tokens)
    scores = jnp.einsum(
        "daq,dak->aqk", shaped[0], shaped[1], preferred_element_type=F32
    ) * HEAD_DIM ** (-0.5)
    weights = jnp.exp(scores)
    weights = (weights / jnp.sum(weights, axis=-1, keepdims=True)).astype(BF16)
    attended = jnp.einsum("dak,aqk->daq", shaped[2], weights, preferred_element_type=F32)
    attended = attended.astype(BF16).reshape(features, column_tokens)
    everyone = from_group(attended, 2).reshape(full_width, column_tokens)
    mixed = tokens + jnp.einsum("fo,fn->on", out_weight, everyone, preferred_element_type=F32)

    route = route_index.T
    slot = slot_index.T
    expert_ids = jnp.arange(experts, dtype=jnp.int32)
    chosen = route[:, None, :] == expert_ids[None, :, None]

    def picked(table):
        return jnp.sum(jnp.where(chosen, table[None], 0.0), axis=1)

    router_rows = router_weight.T
    direct = jnp.dot(
        router_rows * pre_expert_gain[None, :], mixed, precision=lax.Precision.HIGHEST
    )
    gain_scores = jnp.sum(router_rows * pre_expert_gain[None, :], axis=1)
    partial = jnp.concatenate(
        [
            jnp.sum(mixed, axis=0, keepdims=True),
            jnp.sum(mixed * mixed, axis=0, keepdims=True),
            picked(direct),
        ],
        axis=0,
    ).reshape(4 * tiles_here, tile_tokens)
    extra = jnp.broadcast_to(
        jnp.pad(gain_scores, (0, 64 - experts))[None, :], (4 * tiles_here, 64)
    )
    totals = summed(jnp.concatenate([partial, extra], axis=1), 3)
    gain_sum = totals[0, tile_tokens : tile_tokens + experts]
    totals = totals[:, :tile_tokens].reshape(4, column_tokens)
    mean_value = totals[0:1] / full_width
    inverse_std = lax.rsqrt(totals[1:2] / full_width - mean_value * mean_value + 1e-06)
    expert_in = (mixed - mean_value) * inverse_std * pre_expert_gain[:, None]
    expert_in = jnp.where(live[None, :], expert_in, 0.0).astype(BF16)
    logits = inverse_std * (totals[2:4] - mean_value * picked(gain_sum[:, None]))
    gates = jax.nn.sigmoid(logits - logits[::-1])
    keep = slot >= 0
    target = jnp.where(keep, route * stride + slot, -1)
    slot_ids = jnp.arange(experts * stride, dtype=jnp.int32)
    hits = slot_ids[None, :, None] == target[:, None, :]
    chosen_slot = (hits[0] | hits[1]).astype(BF16)
    outbound = jnp.einsum("qn,fn->qf", chosen_slot, expert_in, preferred_element_type=F32)
    outbound = outbound.astype(BF16).reshape(experts, stride, features)
    inbound = exchanged(outbound, 4)
    slots = jnp.transpose(inbound[:, :capacity], (2, 0, 1)).reshape(
        features, expert_count * capacity
    )
    rows_in = from_group(slots, 5).reshape(full_width, expert_count * capacity)
    hidden_pre = jnp.einsum("fs,fh->sh", rows_in, expand_weight[0], preferred_element_type=F32)
    activated = jax.nn.gelu(hidden_pre, approximate=False).astype(BF16)
    partial_out = jnp.einsum(
        "hf,sh->fs", reduce_weight[0], activated, preferred_element_type=F32
    ).astype(BF16)
    expert_sum = sum_at_owner(
        partial_out.reshape(group, features, expert_count * capacity), 6
    )
    returned = jnp.transpose(
        expert_sum.reshape(features, expert_count, capacity), (1, 2, 0)
    )
    returned = jnp.pad(returned, ((0, 0), (0, stride - capacity), (0, 0)))
    fetched = exchanged(returned, 7).reshape(experts * stride, features)
    gates = jnp.where(keep & live[None, :], gates, 0.0)
    mixing = jnp.where(hits[0], gates[0:1], 0.0) + jnp.where(hits[1], gates[1:2], 0.0)
    final = mixed
    for piece in two_parts(mixing):
        final = final + jnp.einsum("qf,qn->fn", fetched, piece, preferred_element_type=F32)
    final = jnp.where(live[None, :], final, 0.0)
    accumulated = 0.0
    for piece in two_parts(final):
        accumulated = accumulated + jnp.einsum(
            "fn,pn->fp", piece, chosen_patch, preferred_element_type=F32
        )
    incoming = passed_along(
        accumulated[:, own_lanes : own_lanes + side_patches].astype(BF16), "expert", 1
    ).astype(F32)
    result = accumulated[:, :own_patches] + jnp.pad(
        incoming, ((0, 0), (0, own_patches - side_patches))
    )
    result = result.astype(BF16).reshape(features, own_width, height)
    return jnp.transpose(result, (2, 1, 0))


def solution(mesh):
    split = Mesh(mesh.devices.reshape(SIDE, SIDE, mesh.shape["expert"]), ("y", "x", "expert"))
    return jax.shard_map(
        body,
        mesh=split,
        in_specs=(
            P(None, "expert", DP),
            P("expert", None),
            P("expert"),
            P(DP),
            P(None, None, DP),
            P(None, DP),
            P(DP),
            P(DP, None),
            P("expert", None, DP),
            P("expert", DP, None),
            P("expert", None),
            P("expert", None),
        ),
        out_specs=P(None, "expert", DP),
        check_vma=False,
    )
```
